1024 devices in a mesh: dom: 64 (over z, core), help: 16 (over y, x).
Axes of the slice: x: 4, y: 4, z: 32, core: 2. Of those that a mesh axis runs over, the one named last changes fastest.
Arguments:
- positions: float32 [3, 64, 16, 3, 256], P(None, 'dom', 'help'), may hold values from 0 to 1
- velocities: float32 [3, 64, 16, 3, 256], P(None, 'dom', 'help'), may hold values from -6 to 6
- masses: float32 [64, 16, 3, 256], P('dom', 'help'), may hold values from 0.5 to 2
- counts: int32 [64, 16, 3], P('dom'), may hold values from 1 to 256, as said below
- neighbours: int32 [64, 16, 3, 27], P('dom'), may hold values from 0 to 2, as said below
Outputs:
- places: float32 [3, 64, 16, 3, 256], P(None, 'dom', 'help')
- speeds: float32 [3, 64, 16, 3, 256], P(None, 'dom', 'help')
The draws below stay inside these ranges and needn't reach their ends.
Inputs may be any that keep to these rules, and one draw needn't show every extreme that they name: `counts`: particles 0 to count - 1 of a bin are live; some bin holds 256. `neighbours`: each column of 3 bins is stored in its own order along y; entry k of bin (x, z, s) is the stored slot of the bin that lies at offset (k // 9 - 1, k % 3 - 1, k // 3 % 3 - 1) along (x, y, z) from it, periodically.
All inputs are finite; a program needn't handle non-finite values.
Results may differ from the reference program's by a relative error of at most 0.00016.
Values sent between devices are 32-bit elements; how exact they have to be, the bound alone decides.
No kernel may reach another device: no remote copies, remote signals or barrier semaphores. Data moves between devices by JAX's collectives and lax.ppermute only.
A program may use at most 32 MiB of HBM per device.

```python
import math
import jax
import jax.numpy as jnp
from jax import lax

P_SIZE = 256
SLOTS = 27
GY = 3
SUBSTEPS = 3
GX = 64
GZ = 16


def pick_order(subkey):
    return jax.random.permutation(subkey, GY)


def column_orders(key):
    keys = jax.random.split(jax.random.fold_in(key, 11), GX * GZ)
    orders = jax.vmap(pick_order)(keys)
    return orders.reshape(GX, GZ, GY).astype(jnp.int32)


def draw_neighbours(key, part):
    orders = column_orders(key)
    inverse = jnp.argsort(orders, axis=-1, stable=True).astype(jnp.int32)
    columns = []
    for slot_index in range(SLOTS):
        along_x = slot_index // 9 - 1
        along_y = slot_index % 3 - 1
        along_z = slot_index // 3 % 3 - 1
        wanted = ((orders + along_y) % GY).astype(jnp.int32)
        moved = jnp.roll(inverse, (-along_x, -along_z), axis=(0, 1))
        columns.append(jnp.take_along_axis(moved, wanted, axis=2))
    return jnp.stack(columns, axis=-1).astype(jnp.int32)


def draw_counts(key, part):
    levels = jax.random.randint(jax.random.fold_in(key, 3), (GX, 1, 1), 1, 17).astype(jnp.int32)
    ceiling = jnp.maximum(levels * P_SIZE // 16, 1).astype(jnp.int32)
    base = jax.random.randint(key, (GX, GZ, GY), 1, P_SIZE + 1).astype(jnp.int32)
    base = (base - 1) % ceiling + 1
    flat = base.reshape(GX * GZ * GY)
    chosen_spot = jax.random.randint(jax.random.fold_in(key, 5), (), 0, GX * GZ * GY)
    filled = jnp.where(jnp.arange(GX * GZ * GY) == chosen_spot, P_SIZE, flat)
    return filled.reshape(GX, GZ, GY).astype(jnp.int32)


def block_levels(stream_key, extent, cuts, smallest, top_value):
    def one(axis_at, shards_of):
        heights = jax.random.uniform(jax.random.fold_in(jax.random.fold_in(stream_key, 6), axis_at), (shards_of,), jnp.float32, smallest / len(cuts), top_value / len(cuts))
        return jnp.repeat(jnp.exp(heights), extent[axis_at] // shards_of).reshape((-1,) + (1,) * (len(extent) - axis_at - 1))

    loudness = one(*cuts[0])
    for cut in cuts[1:]:
        loudness = loudness * one(*cut)
    return loudness


def scatter_about(own_key, shape, width, most, cuts=(), held_as=jnp.bfloat16):
    values = jax.random.normal(own_key, shape, jnp.float32) * width
    if len(cuts) > 0:
        values = block_levels(own_key, shape, cuts, -0.22, 0.18) * values
    return jnp.clip(values, min=-most, max=most).astype(held_as)


def setup_inputs(seed: int = 0) -> dict:
    key_of = jax.random.split(jax.random.key(seed), 6)
    positions = jnp.clip(1.0 * jax.random.uniform(key_of[0], (3, GX, GZ, GY, P_SIZE), jnp.float32) ** block_levels(key_of[0], (3, GX, GZ, GY, P_SIZE), ((1, 64), (2, 16)), -0.2, 0.2), 0.0, 1.0)
    velocities = scatter_about(key_of[1], (3, GX, GZ, GY, P_SIZE), 1.0, 6.0, ((1, 64), (2, 16)), jnp.float32)
    masses = jnp.clip(jnp.exp(math.log(2.0) - 1.3862944 * jax.random.uniform(key_of[2], (GX, GZ, GY, P_SIZE), jnp.float32) ** block_levels(key_of[2], (GX, GZ, GY, P_SIZE), ((0, 64), (1, 16)), -0.2, 0.2)), 0.5, 2.0)
    counts = draw_counts(jax.random.fold_in(key_of[5], 71), 0)
    neighbours = draw_neighbours(jax.random.fold_in(key_of[5], 71), 0)
    return {"positions": positions, "velocities": velocities, "masses": masses, "counts": counts, "neighbours": neighbours}


softening = 0.25
strength = 4.0
time_step = 0.2

def slot_offsets(slot_index):
    return (slot_index // 9 - 1, slot_index % 3 - 1, slot_index // 3 % 3 - 1)

def attract(targets, sources, offset):
    displaced = [sources[c][:, None, :] + offset[c] - targets[c][:, :, None] for c in range(3)]
    squared = displaced[0] * displaced[0] + displaced[1] * displaced[1] + displaced[2] * displaced[2] + softening
    inverse = lax.rsqrt(squared)
    weighting = sources[3][:, None, :] * inverse * inverse * inverse
    return jnp.stack([lax.optimization_barrier(jnp.sum(weighting * component, axis=2)) for component in displaced])

def reference(positions, velocities, masses, counts, neighbours):
    living = (jnp.arange(P_SIZE, dtype=jnp.int32)[None, None, None, :] < counts[..., None]).astype(jnp.float32)
    heavy = masses * living
    choose = (neighbours[..., None] == jnp.arange(GY, dtype=jnp.int32)[None, None, None, None, :]).astype(jnp.float32)
    places, speeds = (positions, velocities)
    for substep in range(SUBSTEPS):
        packet = jnp.concatenate([places, heavy[None]], axis=0)
        padded = jnp.concatenate([packet[:, -1:], packet, packet[:, :1]], axis=1)

        def forces_at(index):
            window = lax.dynamic_slice_in_dim(padded, index, 3, 1)
            targets = lax.dynamic_index_in_dim(places, index, 1, keepdims=False).reshape(3, GZ * GY, P_SIZE)
            picks = lax.dynamic_index_in_dim(choose, index, 0, keepdims=False)
            summed = jnp.zeros((3, GZ * GY, P_SIZE), jnp.float32)
            for slot_index in range(SLOTS):
                offset = slot_offsets(slot_index)
                column = jnp.roll(window[:, 1 + offset[0]], -offset[2], axis=1)
                chosen = jnp.einsum('czsp,zts->cztp', column, picks[:, :, slot_index, :], precision=lax.Precision.HIGHEST)
                summed = summed + attract(targets, chosen.reshape(4, GZ * GY, P_SIZE), (float(offset[0]), float(offset[1]), float(offset[2])))
            return summed.reshape(3, GZ, GY, P_SIZE)
        forces = lax.map(forces_at, jnp.arange(GX, dtype=jnp.int32))
        forces = jnp.moveaxis(forces, 0, 1)
        accel = forces * (strength / P_SIZE) * living[None]
        speeds = speeds + time_step * accel
        places = places + time_step * speeds
    return (places, speeds)
```

```python
import jax
import jax.numpy as jnp
from jax import lax
from jax.experimental import pallas as pl
from jax.experimental.pallas import tpu as pltpu
from jax.sharding import PartitionSpec as P

SUBSTEPS = 3

softening = 0.25
strength = 4.0
time_step = 0.2

ROWS = 8
BLOCK = 256
LANES = 128


def ring(count, shift):
    return [(i, (i + shift) % count) for i in range(count)]


def parts_of(value):
    first = value.astype(jnp.bfloat16).astype(jnp.float32)
    rest = value - first
    second = rest.astype(jnp.bfloat16).astype(jnp.float32)
    return first, second, rest - second


def row_lane(shape):
    return (
        lax.broadcasted_iota(jnp.int32, shape, 0),
        lax.broadcasted_iota(jnp.int32, shape, 1),
    )


Y_ROWS = (1, 4, 5)


def bin_of_lane(lane, slots):
    return jnp.where(lane < slots, 0, jnp.where(lane < 2 * slots, 1, 2))


def own_y_row(row, bin_of):
    return row == jnp.where(bin_of == 0, Y_ROWS[0], jnp.where(bin_of == 1, Y_ROWS[1], Y_ROWS[2]))


def is_y_row(row):
    return (row == Y_ROWS[0]) | (row == Y_ROWS[1]) | (row == Y_ROWS[2])


def pack_kernel(
    counts_ref, links_ref, helper_ref, places_ref, speeds_ref, masses_ref, packet_ref, speed_ref, moves_ref
):
    helper = helper_ref[0]
    row, lane = row_lane((ROWS, LANES))
    pieces = places_ref.shape[0] // 3
    per_bin = pieces // 3
    for piece in range(pieces):
        b = piece // per_bin
        count = counts_ref[b, 0, helper]
        span = slice(piece * LANES, (piece + 1) * LANES)
        for c in range(3):
            packet_ref[c : c + 1, span] = places_ref[c * pieces + piece]
            speed_ref[c : c + 1, span] = speeds_ref[c * pieces + piece]
        packet_ref[3:4, span] = jnp.where(
            lane[:1] + piece % per_bin * LANES < count, masses_ref[piece], 0.0
        )
        speed_ref[3:4, span] = jnp.zeros((1, LANES), jnp.float32)
    for column in range(9):
        dx, dz = column // 3 - 1, column % 3 - 1
        side = jnp.where(row == 0, float(dx), jnp.where(row == 2, float(dz), 0.0))
        for q in range(3):
            move = side
            for s, y_row in enumerate(Y_ROWS):
                step = jnp.where(
                    links_ref[s, helper, 3 * column] == q,
                    -1.0,
                    jnp.where(links_ref[s, helper, 3 * column + 2] == q, 1.0, 0.0),
                )
                move = jnp.where(row == y_row, step, move)
            index = 3 * column + q
            moves_ref[:, index * LANES : (index + 1) * LANES] = move


def spread(packet):
    return jnp.concatenate([packet, jnp.broadcast_to(packet[1:2], packet.shape)], axis=0)


def gather_sources(columns, moves_ref, packed_ref, slots):
    _, lane = row_lane((ROWS, LANES))
    filled = jnp.int32(0)
    base = jnp.int32(0)
    for ref, column in columns:
        for q in range(3):
            heavy = ref[3:4, q * slots : (q + 1) * slots]
            count = jnp.sum(jnp.where(heavy > 0.0, 1.0, 0.0)).astype(jnp.int32)
            move = moves_ref[:, pl.ds(pl.multiple_of((3 * column + q) * LANES, LANES), LANES)]
            shift = filled & (LANES - 1)
            base = pl.multiple_of(filled - shift, LANES)
            keep = lane < shift
            old = packed_ref[:, pl.ds(base, LANES)]
            for piece in range(slots // LANES):
                start = q * slots + piece * LANES
                new = pltpu.roll(spread(ref[:, start : start + LANES]) + move, shift, 1)
                packed_ref[:, pl.ds(base + piece * LANES, LANES)] = jnp.where(keep, old, new)
                old = new
            packed_ref[:, pl.ds(base + slots, LANES)] = jnp.where(keep, old, 0.0)
            filled = filled + count
    for piece in range(1, 3):
        packed_ref[:, pl.ds(base + slots + piece * LANES, LANES)] = jnp.zeros(
            (ROWS, LANES), jnp.float32
        )
    return filled


def target_matrix(packet, slots):
    packet = spread(packet)
    row, lane = row_lane(packet.shape)
    mine = own_y_row(row, bin_of_lane(lane, slots))
    t1, t2, t3 = parts_of(jnp.where((row == 0) | (row == 2) | mine, -2.0 * packet, 0.0))
    x, y, z = packet[0:1], packet[1:2], packet[2:3]
    u1, u2, u3 = parts_of(x * x + y * y + z * z + softening)
    ones = jnp.where(mine, 1.0, 0.0)
    last = jnp.where(row == 0, u1, jnp.where(row == 1, u2, jnp.where(row == 2, u3, 0.0)))
    return jnp.concatenate([t1, t1, t2, t1, t2, t3, ones, ones, ones, last], axis=0).astype(
        jnp.bfloat16
    )


def add_sources(filled, packed_ref, target_ref, sum_ref, source_ref, moment_ref):
    row, _ = row_lane((ROWS, BLOCK))

    def prepare(index):
        start = pl.multiple_of(index * BLOCK, BLOCK)
        block = packed_ref[:, pl.ds(start, BLOCK)]
        s1, s2, s3 = parts_of(block)
        squares = block * block
        q1, q2, q3 = parts_of(squares + (squares[0:1] + squares[2:3]))
        ones = jnp.ones((ROWS, BLOCK), jnp.float32)
        rows = jnp.concatenate([s1, s2, s1, s3, s2, s1, q1, q2, q3, ones], axis=0)
        moment = jnp.where(row == 3, block, block * block[3:4])
        m1, m2, m3 = parts_of(moment)
        moments = jnp.concatenate([m1, m2, m3, jnp.zeros_like(m1)], axis=0)
        return rows.astype(jnp.bfloat16).T, moments.astype(jnp.bfloat16)

    def step(index, carry):
        moments = moment_ref[...]
        squared = jnp.dot(source_ref[...], target_ref[...], preferred_element_type=jnp.float32)
        inverse = lax.rsqrt(squared)
        weight = inverse * inverse * inverse
        high = weight.astype(jnp.bfloat16)
        low = (weight - high.astype(jnp.float32)).astype(jnp.bfloat16)
        sum_ref[...] += jnp.dot(moments, high, preferred_element_type=jnp.float32) + jnp.dot(
            moments, low, preferred_element_type=jnp.float32
        )
        source_ref[...], moment_ref[...] = prepare(index + 1)
        return carry

    sum_ref[...] = jnp.zeros_like(sum_ref)
    source_ref[...], moment_ref[...] = prepare(0)
    lax.fori_loop(0, (filled + BLOCK - 1) >> (BLOCK.bit_length() - 1), step, 0)
    return sum_ref[0:ROWS] + sum_ref[ROWS : 2 * ROWS] + sum_ref[2 * ROWS : 3 * ROWS]


def updated(packet, speed, total, slots):
    row, lane = row_lane(packet.shape)
    bin_of = bin_of_lane(lane[:1], slots)
    x, y, z = packet[0:1], packet[1:2], packet[2:3]
    all_mass = total[3:4]
    total_y = jnp.where(bin_of == 0, total[1:2], jnp.where(bin_of == 1, total[4:5], total[5:6]))
    pull_x, pull_y, pull_z = (
        total[0:1] - x * all_mass,
        total_y - y * all_mass,
        total[2:3] - z * all_mass,
    )
    force = jnp.where(row == 0, pull_x, jnp.where(row == 1, pull_y, pull_z))
    living = (packet[3:4] > 0.0) & (row < 3)
    accel = jnp.where(living, force * (strength / slots), 0.0)
    speed = speed + time_step * accel
    return packet + time_step * speed, speed


def own_kernel(slots, moves_ref, packet_ref, target_ref, total_ref, packed_ref, *work):
    target_ref[...] = target_matrix(packet_ref[...], slots)
    filled = gather_sources([(packet_ref, 4)], moves_ref, packed_ref, slots)
    total_ref[...] = add_sources(filled, packed_ref, target_ref, *work)


def side_kernel(
    slots, helper_ref, moves_ref, even_ref, odd_ref, target_ref, total_ref, out_ref, packed_ref, *work
):
    turn = 1 - 2 * (helper_ref[0] & 1)
    columns = [(even_ref, 4 + turn), (odd_ref, 4 - turn)]
    filled = gather_sources(columns, moves_ref, packed_ref, slots)
    out_ref[...] = total_ref[...] + add_sources(filled, packed_ref, target_ref, *work)


def far_kernel(slots, last, helper_ref, moves_ref, packet_ref, before_ref, after_ref, speed_ref, target_ref, total_ref, *rest):
    first_out, second_out, packed_ref, *work = rest
    turn = 1 - 2 * (helper_ref[0] & 1)
    columns = [
        (ref.at[place], column + dz)
        for ref, column in ((before_ref, 1), (after_ref, 7))
        for place, dz in enumerate((turn, 0, -turn))
    ]
    filled = gather_sources(columns, moves_ref, packed_ref, slots)
    total = total_ref[...] + add_sources(filled, packed_ref, target_ref, *work)
    packet, speed = updated(packet_ref[...], speed_ref[...], total, slots)
    if last:
        pieces = first_out.shape[0] // 3
        for c in range(3):
            for piece in range(pieces):
                span = slice(piece * LANES, (piece + 1) * LANES)
                first_out[c * pieces + piece] = packet[c : c + 1, span]
                second_out[c * pieces + piece] = speed[c : c + 1, span]
    else:
        first_out[...] = packet
        second_out[...] = speed


def near_memory(value):
    return pltpu.with_memory_space_constraint(value, pltpu.VMEM)


def work_space(columns, width, slots):
    return [
        pltpu.VMEM((ROWS, columns * width + 3 * slots), jnp.float32),
        pltpu.VMEM((4 * ROWS, width), jnp.float32),
        pltpu.VMEM((BLOCK, 10 * ROWS), jnp.bfloat16),
        pltpu.VMEM((4 * ROWS, BLOCK), jnp.bfloat16),
    ]


def on_device(positions, velocities, masses, counts, neighbours):
    bins, slots = positions.shape[3], positions.shape[4]
    width = bins * slots
    pieces = width // LANES
    helper = lax.axis_index("help").reshape(1).astype(jnp.int32)
    vmem = pl.BlockSpec(memory_space=pltpu.VMEM)
    smem = pl.BlockSpec(memory_space=pltpu.SMEM)
    state = pltpu.VMEM((4, width), jnp.float32)
    packet, speed, moves = pl.pallas_call(
        pack_kernel,
        out_shape=(state, state, pltpu.VMEM((ROWS, 27 * LANES), jnp.float32)),
        in_specs=[smem, smem, smem, vmem, vmem, vmem],
        out_specs=(vmem, vmem, vmem),
        name="pack",
    )(
        counts.transpose(2, 0, 1),
        neighbours[0].transpose(1, 0, 2),
        helper,
        positions.reshape(3 * pieces, 1, LANES),
        velocities.reshape(3 * pieces, 1, LANES),
        masses.reshape(pieces, 1, LANES),
    )
    doms, helpers = lax.axis_size("dom"), lax.axis_size("help")
    even = [(i, i ^ 1) for i in range(helpers)]
    odd = [(i, (i + 1) % helpers if i % 2 else (i - 1) % helpers) for i in range(helpers)]
    final = jax.ShapeDtypeStruct((3 * pieces, 1, LANES), jnp.float32)

    target_shape = pltpu.VMEM((10 * ROWS, width), jnp.bfloat16)
    total_shape = pltpu.VMEM((ROWS, width), jnp.float32)
    cost = pl.CostEstimate(flops=10**9, transcendentals=10**6, bytes_accessed=10**6)

    def own(*refs):
        own_kernel(slots, *refs)

    def side(*refs):
        side_kernel(slots, *refs)

    for substep in range(SUBSTEPS):
        last = substep == SUBSTEPS - 1

        def far(*refs, last=last):
            far_kernel(slots, last, *refs)

        across = lax.ppermute(packet, "help", even)
        beyond = lax.ppermute(packet, "help", odd)
        target, total = pl.pallas_call(
            own,
            out_shape=(target_shape, total_shape),
            in_specs=[vmem, vmem],
            out_specs=(vmem, vmem),
            scratch_shapes=work_space(1, width, slots),
            cost_estimate=cost,
            name="own",
        )(near_memory(moves), near_memory(packet))
        slab = jnp.stack([across, packet, beyond])
        before = lax.ppermute(slab, "dom", ring(doms, 1))
        after = lax.ppermute(slab, "dom", ring(doms, -1))
        total = pl.pallas_call(
            side,
            out_shape=total_shape,
            in_specs=[smem] + [vmem] * 5,
            out_specs=vmem,
            scratch_shapes=work_space(2, width, slots),
            cost_estimate=cost,
            name="side",
        )(
            helper,
            near_memory(moves),
            near_memory(across),
            near_memory(beyond),
            near_memory(target),
            near_memory(total),
        )
        packet, speed = pl.pallas_call(
            far,
            out_shape=(final, final) if last else (state, state),
            in_specs=[smem] + [vmem] * 7,
            out_specs=(vmem, vmem),
            scratch_shapes=work_space(6, width, slots),
            cost_estimate=cost,
            name="far_last" if last else "far",
        )(
            helper,
            near_memory(moves),
            near_memory(packet),
            near_memory(before),
            near_memory(after),
            near_memory(speed),
            near_memory(target),
            near_memory(total),
        )
    return packet.reshape(positions.shape), speed.reshape(positions.shape)


def solution(mesh):
    return jax.shard_map(
        on_device,
        mesh=mesh,
        in_specs=(
            P(None, "dom", "help", None, None),
            P(None, "dom", "help", None, None),
            P("dom", "help", None, None),
            P("dom", None, None),
            P("dom", None, None, None),
        ),
        out_specs=(P(None, "dom", "help", None, None), P(None, "dom", "help", None, None)),
        check_vma=False,
    )
```

```python
import functools

import jax
import jax.numpy as jnp
from jax import lax
from jax.experimental import pallas as pl
from jax.experimental.pallas import tpu as pltpu
from jax.sharding import PartitionSpec as P


SUBSTEPS = 3

softening = 0.25
strength = 4.0
time_step = 0.2

ROWS = 8
BLOCK = 256
LANES = 128


def ring(count, shift):
    return [(i, (i + shift) % count) for i in range(count)]


def parts_of(value):
    first = value.astype(jnp.bfloat16).astype(jnp.float32)
    rest = value - first
    second = rest.astype(jnp.bfloat16).astype(jnp.float32)
    return first, second, rest - second


def row_lane(shape):
    return (
        lax.broadcasted_iota(jnp.int32, shape, 0),
        lax.broadcasted_iota(jnp.int32, shape, 1),
    )


Y_ROWS = (1, 4, 5)


def bin_of_lane(lane, slots):
    return jnp.where(lane < slots, 0, jnp.where(lane < 2 * slots, 1, 2))


def own_y_row(row, bin_of):
    return row == jnp.where(bin_of == 0, Y_ROWS[0], jnp.where(bin_of == 1, Y_ROWS[1], Y_ROWS[2]))


def pack_kernel(
    counts_ref, links_ref, helper_ref, places_ref, speeds_ref, masses_ref, packet_ref, speed_ref, moves_ref
):
    helper = helper_ref[0]
    row, lane = row_lane((ROWS, LANES))
    pieces = places_ref.shape[0] // 3
    per_bin = pieces // 3
    for piece in range(pieces):
        b = piece // per_bin
        count = counts_ref[b, 0, helper]
        span = slice(piece * LANES, (piece + 1) * LANES)
        for c in range(3):
            packet_ref[c : c + 1, span] = places_ref[c * pieces + piece]
            speed_ref[c : c + 1, span] = speeds_ref[c * pieces + piece]
        packet_ref[3:4, span] = jnp.where(
            lane[:1] + piece % per_bin * LANES < count, masses_ref[piece], 0.0
        )
        speed_ref[3:4, span] = jnp.zeros((1, LANES), jnp.float32)
    for column in range(9):
        dx, dz = column // 3 - 1, column % 3 - 1
        side = jnp.where(row == 0, float(dx), jnp.where(row == 2, float(dz), 0.0))
        for q in range(3):
            move = side
            for s, y_row in enumerate(Y_ROWS):
                step = jnp.where(
                    links_ref[s, helper, 3 * column] == q,
                    -1.0,
                    jnp.where(links_ref[s, helper, 3 * column + 2] == q, 1.0, 0.0),
                )
                move = jnp.where(row == y_row, step, move)
            index = 3 * column + q
            moves_ref[:, index * LANES : (index + 1) * LANES] = move


def spread(packet):
    return jnp.concatenate([packet, jnp.broadcast_to(packet[1:2], packet.shape)], axis=0)


def gather_sources(columns, moves_ref, packed_ref, slots):
    _, lane = row_lane((ROWS, LANES))
    filled = jnp.int32(0)
    base = jnp.int32(0)
    for ref, column in columns:
        for q in range(3):
            heavy = ref[3:4, q * slots : (q + 1) * slots]
            count = jnp.sum(jnp.where(heavy > 0.0, 1.0, 0.0)).astype(jnp.int32)
            move = moves_ref[:, pl.ds(pl.multiple_of((3 * column + q) * LANES, LANES), LANES)]
            shift = filled & (LANES - 1)
            base = pl.multiple_of(filled - shift, LANES)
            keep = lane < shift
            old = packed_ref[:, pl.ds(base, LANES)]
            for piece in range(slots // LANES):
                start = q * slots + piece * LANES
                new = pltpu.roll(spread(ref[:, start : start + LANES]) + move, shift, 1)
                packed_ref[:, pl.ds(base + piece * LANES, LANES)] = jnp.where(keep, old, new)
                old = new
            packed_ref[:, pl.ds(base + slots, LANES)] = jnp.where(keep, old, 0.0)
            filled = filled + count
    for piece in range(1, 3):
        packed_ref[:, pl.ds(base + slots + piece * LANES, LANES)] = jnp.zeros(
            (ROWS, LANES), jnp.float32
        )
    return filled


def target_matrix(packet, slots):
    packet = spread(packet)
    row, lane = row_lane(packet.shape)
    mine = own_y_row(row, bin_of_lane(lane, slots))
    t1, t2, t3 = parts_of(jnp.where((row == 0) | (row == 2) | mine, -2.0 * packet, 0.0))
    x, y, z = packet[0:1], packet[1:2], packet[2:3]
    u1, u2, u3 = parts_of(x * x + y * y + z * z + softening)
    ones = jnp.where(mine, 1.0, 0.0)
    last = jnp.where(row == 0, u1, jnp.where(row == 1, u2, jnp.where(row == 2, u3, 0.0)))
    return jnp.concatenate([t1, t1, t2, t1, t2, t3, ones, ones, ones, last], axis=0).astype(
        jnp.bfloat16
    )


def add_sources(filled, packed_ref, target_ref, sum_ref):
    def step(first, size, index, carry):
        start = pl.multiple_of(first * BLOCK + index * size, BLOCK)
        block = packed_ref[:, pl.ds(start, size)]
        row, _ = row_lane(block.shape)
        s1, s2, s3 = parts_of(block)
        squares = block * block
        q1, q2, q3 = parts_of(squares + (squares[0:1] + squares[2:3]))
        ones = jnp.ones(block.shape, jnp.float32)
        rows = jnp.concatenate([s1, s2, s1, s3, s2, s1, q1, q2, q3, ones], axis=0)
        sources = rows.astype(jnp.bfloat16).T
        squared = jnp.dot(sources, target_ref[...], preferred_element_type=jnp.float32)
        inverse = lax.rsqrt(squared)
        weight = inverse * inverse * inverse
        high = weight.astype(jnp.bfloat16)
        low = (weight - high.astype(jnp.float32)).astype(jnp.bfloat16)
        moment = jnp.where(row == 3, block, block * block[3:4])
        m1, m2, m3 = parts_of(moment)
        moments = jnp.concatenate([m1, m2, m3, jnp.zeros_like(m1)], axis=0).astype(jnp.bfloat16)
        sum_ref[...] += jnp.dot(moments, high, preferred_element_type=jnp.float32) + jnp.dot(
            moments, low, preferred_element_type=jnp.float32
        )
        return carry

    sum_ref[...] = jnp.zeros_like(sum_ref)
    count = (filled + BLOCK - 1) >> (BLOCK.bit_length() - 1)
    lax.fori_loop(0, count >> 1, functools.partial(step, 0, 2 * BLOCK), 0)
    lax.fori_loop(0, count & 1, functools.partial(step, count - 1, BLOCK), 0)
    return sum_ref[0:ROWS] + sum_ref[ROWS : 2 * ROWS] + sum_ref[2 * ROWS : 3 * ROWS]


def updated(packet, speed, total, slots):
    row, lane = row_lane(packet.shape)
    bin_of = bin_of_lane(lane[:1], slots)
    x, y, z = packet[0:1], packet[1:2], packet[2:3]
    all_mass = total[3:4]
    total_y = jnp.where(bin_of == 0, total[1:2], jnp.where(bin_of == 1, total[4:5], total[5:6]))
    pull_x, pull_y, pull_z = (
        total[0:1] - x * all_mass,
        total_y - y * all_mass,
        total[2:3] - z * all_mass,
    )
    force = jnp.where(row == 0, pull_x, jnp.where(row == 1, pull_y, pull_z))
    living = (packet[3:4] > 0.0) & (row < 3)
    accel = jnp.where(living, force * (strength / slots), 0.0)
    speed = speed + time_step * accel
    return packet + time_step * speed, speed


def own_kernel(slots, moves_ref, packet_ref, target_ref, total_ref, packed_ref, *work):
    target_ref[...] = target_matrix(packet_ref[...], slots)
    filled = gather_sources([(packet_ref, 4)], moves_ref, packed_ref, slots)
    total_ref[...] = add_sources(filled, packed_ref, target_ref, *work)


def side_kernel(
    slots, helper_ref, moves_ref, even_ref, odd_ref, target_ref, total_ref, out_ref, packed_ref, *work
):
    turn = 1 - 2 * (helper_ref[0] & 1)
    columns = [(even_ref, 4 + turn), (odd_ref, 4 - turn)]
    filled = gather_sources(columns, moves_ref, packed_ref, slots)
    out_ref[...] = total_ref[...] + add_sources(filled, packed_ref, target_ref, *work)


def far_kernel(slots, last, helper_ref, moves_ref, packet_ref, before_ref, after_ref, speed_ref, target_ref, total_ref, *rest):
    first_out, second_out, packed_ref, *work = rest
    turn = 1 - 2 * (helper_ref[0] & 1)
    columns = [
        (ref.at[place], column + dz)
        for ref, column in ((before_ref, 1), (after_ref, 7))
        for place, dz in enumerate((turn, 0, -turn))
    ]
    filled = gather_sources(columns, moves_ref, packed_ref, slots)
    total = total_ref[...] + add_sources(filled, packed_ref, target_ref, *work)
    packet, speed = updated(packet_ref[...], speed_ref[...], total, slots)
    if last:
        pieces = first_out.shape[0] // 3
        for c in range(3):
            for piece in range(pieces):
                span = slice(piece * LANES, (piece + 1) * LANES)
                first_out[c * pieces + piece] = packet[c : c + 1, span]
                second_out[c * pieces + piece] = speed[c : c + 1, span]
    else:
        first_out[...] = packet
        second_out[...] = speed


def near_memory(value):
    return pltpu.with_memory_space_constraint(value, pltpu.VMEM)


def work_space(columns, width, slots):
    return [
        pltpu.VMEM((ROWS, columns * width + 3 * slots), jnp.float32),
        pltpu.VMEM((4 * ROWS, width), jnp.float32),
    ]


def on_device(positions, velocities, masses, counts, neighbours):
    bins, slots = positions.shape[3], positions.shape[4]
    width = bins * slots
    pieces = width // LANES
    helper = lax.axis_index("help").reshape(1).astype(jnp.int32)
    vmem = pl.BlockSpec(memory_space=pltpu.VMEM)
    smem = pl.BlockSpec(memory_space=pltpu.SMEM)
    state = pltpu.VMEM((4, width), jnp.float32)
    packet, speed, moves = pl.pallas_call(
        pack_kernel,
        out_shape=(state, state, pltpu.VMEM((ROWS, 27 * LANES), jnp.float32)),
        in_specs=[smem, smem, smem, vmem, vmem, vmem],
        out_specs=(vmem, vmem, vmem),
        name="pack",
    )(
        counts.transpose(2, 0, 1),
        neighbours[0].transpose(1, 0, 2),
        helper,
        positions.reshape(3 * pieces, 1, LANES),
        velocities.reshape(3 * pieces, 1, LANES),
        masses.reshape(pieces, 1, LANES),
    )
    doms, helpers = lax.axis_size("dom"), lax.axis_size("help")
    even = [(i, i ^ 1) for i in range(helpers)]
    odd = [(i, (i + 1) % helpers if i % 2 else (i - 1) % helpers) for i in range(helpers)]
    final = jax.ShapeDtypeStruct((3 * pieces, 1, LANES), jnp.float32)

    target_shape = pltpu.VMEM((10 * ROWS, width), jnp.bfloat16)
    total_shape = pltpu.VMEM((ROWS, width), jnp.float32)
    cost = pl.CostEstimate(flops=10**9, transcendentals=10**6, bytes_accessed=10**6)

    def own(*refs):
        own_kernel(slots, *refs)

    def side(*refs):
        side_kernel(slots, *refs)

    for substep in range(SUBSTEPS):
        last = substep == SUBSTEPS - 1

        def far(*refs, last=last):
            far_kernel(slots, last, *refs)

        beyond = lax.ppermute(packet, "help", odd)
        across = lax.ppermute(packet, "help", even)
        target, total = pl.pallas_call(
            own,
            out_shape=(target_shape, total_shape),
            in_specs=[vmem, vmem],
            out_specs=(vmem, vmem),
            scratch_shapes=work_space(1, width, slots),
            cost_estimate=cost,
            name="own",
        )(near_memory(moves), near_memory(packet))
        slab = jnp.stack([across, packet, beyond])
        before = lax.ppermute(slab, "dom", ring(doms, 1))
        after = lax.ppermute(slab, "dom", ring(doms, -1))
        total = pl.pallas_call(
            side,
            out_shape=total_shape,
            in_specs=[smem] + [vmem] * 5,
            out_specs=vmem,
            scratch_shapes=work_space(2, width, slots),
            cost_estimate=cost,
            name="side",
        )(
            helper,
            near_memory(moves),
            near_memory(across),
            near_memory(beyond),
            near_memory(target),
            near_memory(total),
        )
        packet, speed = pl.pallas_call(
            far,
            out_shape=(final, final) if last else (state, state),
            in_specs=[smem] + [vmem] * 7,
            out_specs=(vmem, vmem),
            scratch_shapes=work_space(6, width, slots),
            cost_estimate=cost,
            name="far_last" if last else "far",
        )(
            helper,
            near_memory(moves),
            near_memory(packet),
            near_memory(before),
            near_memory(after),
            near_memory(speed),
            near_memory(target),
            near_memory(total),
        )
    return packet.reshape(positions.shape), speed.reshape(positions.shape)


def solution(mesh):
    return jax.shard_map(
        on_device,
        mesh=mesh,
        in_specs=(
            P(None, "dom", "help", None, None),
            P(None, "dom", "help", None, None),
            P("dom", "help", None, None),
            P("dom", None, None),
            P("dom", None, None, None),
        ),
        out_specs=(P(None, "dom", "help", None, None), P(None, "dom", "help", None, None)),
        check_vma=False,
    )
```
